256 devices in a mesh: chol: 64 (over x_lo, z, y), walk: 4 (over x_hi, core).
Axes of the slice: x: 4 (x_hi: 2, x_lo: 2; x = x_hi * 2 + x_lo), y: 4, z: 8, core: 2. Of those that a mesh axis runs over, the one named last changes fastest.
Arguments:
- green: bfloat16 [256, 128, 512], P(('chol', 'walk')), may hold values from -2 to 2
- cholesky_rotated_vectors: bfloat16 [256, 128, 512], P('chol'), may hold values from -0.25 to 0.25
- walker_weight: float32 [256], P(('chol', 'walk')), may hold values from 0.04 to 0.16
Outputs:
- green_cot: float32 [256, 128, 512], P(('chol', 'walk'))
- chol_grad: float32 [256, 128, 512], P('chol', None, 'walk')
The draws below stay inside these ranges and needn't reach their ends.
All inputs are finite; a program needn't handle non-finite values.
Results may differ from the reference program's by a relative error of at most 0.0029.
Values may be sent and summed in bfloat16 or wider, within the bound.
No kernel may reach another device: no remote copies, remote signals or barrier semaphores. Data moves between devices by JAX's collectives and lax.ppermute only.
A program may use at most 64 MiB of HBM per device.

```python
import math
import jax
import jax.numpy as jnp
from jax import lax

O = 128
M = 512
NV = 256
WALKERS = 256


def levels(rng, extent, split, low, top_value):
    factor_of = 1.0
    for dim, parts in split:
        heights = jax.random.uniform(jax.random.fold_in(jax.random.fold_in(rng, 6), dim), (parts,), jnp.float32, low / len(split), top_value / len(split))
        factor_of = factor_of * jnp.repeat(jnp.exp(heights), extent[dim] // parts).reshape((-1,) + (1,) * (len(extent) - 1 - dim))
    return factor_of


def normal_values(key, shape, deviation, bound, pieces=(), held_as=jnp.bfloat16):
    entries = deviation * jax.random.normal(key, shape, jnp.float32)
    if pieces:
        entries = entries * levels(key, shape, pieces, -0.22, 0.18)
    return jnp.clip(entries, -bound, bound).astype(held_as)


def setup_inputs(seed: int = 0) -> dict:
    streams_of = jax.random.split(jax.random.key(seed), 4)
    green = normal_values(streams_of[0], (WALKERS, O, M), 0.35, 2.0, ((0, 256),))
    cholesky_rotated_vectors = normal_values(streams_of[1], (NV, O, M), M ** -0.5, 0.25, ((0, 64),))
    walker_weight = jnp.clip(jnp.exp(math.log(0.16) - 1.3862944 * jax.random.uniform(streams_of[2], (WALKERS,), jnp.float32) ** levels(streams_of[2], (WALKERS,), ((0, 256),), -0.2, 0.2)), 0.04, 0.16)
    return dict(green=green, cholesky_rotated_vectors=cholesky_rotated_vectors, walker_weight=walker_weight)


def reference(green, cholesky_rotated_vectors, walker_weight):
    chol_float = cholesky_rotated_vectors.astype(jnp.float32)

    def one_walker(chol_sum, input_tuple):
        walker_green_matrix, weight = input_tuple
        green_float = walker_green_matrix.astype(jnp.float32)
        exchange_block = jnp.einsum("gim,jm->gij", chol_float, green_float)
        exchange_block = lax.optimization_barrier(exchange_block.astype(jnp.bfloat16)).astype(jnp.float32)
        green_term = -weight * jnp.einsum("gij,gjm->im", exchange_block, chol_float)
        chol_sum = chol_sum - weight * jnp.einsum("gji,jm->gim", exchange_block, green_float)
        return chol_sum, green_term

    zero_grad = jnp.zeros(cholesky_rotated_vectors.shape, jnp.float32)
    chol_sum, green_terms = lax.scan(one_walker, zero_grad, (green, walker_weight))
    return green_terms, chol_sum
```

```python
import jax
import jax.numpy as jnp
from jax import lax
from jax.experimental import pallas as pl
from jax.experimental.pallas import tpu as pltpu
from jax.sharding import Mesh, PartitionSpec as P

F32 = jnp.float32
BF16 = jnp.bfloat16
AXES = ("xl", "z", "y", "xh", "core")
PLANE = ("xl", "y", "xh")
VMEM = pl.BlockSpec(memory_space=pltpu.VMEM)
HBM = pl.BlockSpec(memory_space=pltpu.HBM)
SMEM = pl.BlockSpec(memory_space=pltpu.SMEM)
EARLY = (0, 1, 7, 2)
LATE = (6, 3, 5, 4)
EXTRA = 16


def shift(block, axis, distance):
    n = lax.axis_size(axis)
    return lax.ppermute(block, axis, [(i, (i + distance) % n) for i in range(n)])


def hold(x):
    return pltpu.with_memory_space_constraint(x, pltpu.HBM)


def call(body, outs, ins, name, mib, flops=0, moved=2 << 20, scratch=(), out_specs=None):
    return pl.pallas_call(
        body,
        out_shape=outs,
        in_specs=ins,
        out_specs=jax.tree.map(lambda _: VMEM, outs) if out_specs is None else out_specs,
        scratch_shapes=scratch,
        compiler_params=pltpu.CompilerParams(vmem_limit_bytes=mib << 20),
        cost_estimate=pl.CostEstimate(flops=flops, bytes_accessed=moved, transcendentals=0),
        name=name,
    )


def prepare(position, weight, green, vectors, payload, spread, own, staged, sems):
    o, m = own.shape
    index = 2 * position[1] + position[0]
    load = pltpu.make_async_copy(vectors.at[index], own, sems.at[0])
    load.start()
    fetch = pltpu.make_async_copy(green.at[0], staged.at[pl.ds(0, o)], sems.at[1])
    fetch.start()
    w = jnp.full((EXTRA, m), weight[0], F32)
    high = w.astype(BF16).astype(F32)
    middle = (w - high).astype(BF16).astype(F32)
    low = w - high - middle
    row = lax.broadcasted_iota(jnp.int32, w.shape, 0)
    tile = jnp.where(row == 0, high, jnp.where(row == 1, middle, jnp.where(row == 2, low, 0.0)))
    staged[o:, :] = tile.astype(BF16)
    load.wait()
    stores = [pltpu.make_async_copy(own, spread.at[k], sems.at[2 + k]) for k in range(spread.shape[0])]
    for copy in stores:
        copy.start()
    fetch.wait()
    stores.append(pltpu.make_async_copy(staged, payload, sems.at[1]))
    stores[-1].start()
    for copy in stores:
        copy.wait()


def gather_line(own):
    up1, down1 = shift(own, "z", 1), shift(own, "z", -1)
    up2, down2 = shift(own, "z", 2), shift(own, "z", -2)
    up3, down3 = shift(up2, "z", 1), shift(down2, "z", -1)
    cut = 80
    far = jnp.concatenate([shift(up2[:cut], "z", 2), shift(down2[cut:], "z", -2)])
    return {0: own, 1: up1, 7: down1, 2: up2, 6: down2, 3: up3, 5: down3, 4: far}


def exchange(
    vectors, mine0, mine1, theirs0, theirs1, exch_mine, exch_theirs, scaled, cot_mine, cot_theirs, greens, cot, sems
):
    m = vectors.shape[1]
    half = mine0.shape[0]
    o = mine0.shape[1] - EXTRA
    count = vectors.shape[0] // o
    quad = 4
    loads = []
    for a, green in enumerate((mine0, mine1, theirs0, theirs1)):
        loads.append(pltpu.make_async_copy(green, greens.at[a], sems.at[a]))
        loads[-1].start()
    for a in range(4):
        exch, base = (exch_mine, exch_theirs)[a // 2], (a % 2) * half
        loads[a].wait()

        @pl.loop(0, half // 2)
        def _(i):
            blocks = [greens[a, 2 * i + w, :o, :] for w in range(2)]
            both = jnp.concatenate(blocks)
            for q in range(count // quad):
                part = lax.dot_general(
                    vectors[q * quad * o : (q + 1) * quad * o, :],
                    both,
                    (((1,), (1,)), ((), ())),
                    preferred_element_type=F32,
                ).astype(BF16)
                for g in range(quad):
                    for w in range(2):
                        exch[
                            pl.ds((base + 2 * i + w) * o, o), (q * quad + g) * o : (q * quad + g + 1) * o
                        ] = part[g * o : (g + 1) * o, w * o : (w + 1) * o]
            for w in range(2):
                weight = jnp.sum(greens[a, 2 * i + w, o:, :].astype(F32), axis=0, keepdims=True)
                rows = (blocks[w].astype(F32) * weight).astype(BF16)
                scaled[a * half // 2 + i, :, w * o : (w + 1) * o] = rows.T

    run = 4 * o
    stores = []
    for r in range(exch_theirs.shape[0] // run):
        rows = slice(r * run, (r + 1) * run)
        cot[rows, :] = jnp.dot(exch_theirs[rows, :], vectors[...], preferred_element_type=F32).astype(BF16)
        stores.append(pltpu.make_async_copy(cot.at[rows], cot_theirs.at[rows], sems.at[4 + r]))
        stores[-1].start()
    for r in range(exch_mine.shape[0] // run):
        rows = slice(r * run, (r + 1) * run)
        cot_mine[rows, :] = jnp.dot(exch_mine[rows, :], vectors[...], preferred_element_type=F32)
    for copy in stores:
        copy.wait()


def gradient(exch_mine, exch_theirs, scaled, grad, staged, sems):
    pairs, m, two = scaled.shape
    columns = exch_mine.shape[1]
    width = 2 * two
    stores = []
    for c in range(columns // width):
        acc = jnp.zeros((m, width), F32)
        for i in range(pairs):
            exch = exch_mine if i < pairs // 2 else exch_theirs
            row = (i % (pairs // 2)) * two
            acc += jnp.dot(
                scaled[i], exch[row : row + two, c * width : (c + 1) * width], preferred_element_type=F32
            )
        acc = acc.astype(BF16)
        for s in range(width // two):
            for h in range(2):
                staged[(c * width // two + s) * 2 + h] = acc[h * m // 2 : (h + 1) * m // 2, s * two : (s + 1) * two]
        span = pl.ds(c * 4, 4)
        stores.append(pltpu.make_async_copy(staged.at[span], grad.at[span], sems.at[c]))
        stores[-1].start()
    for copy in stores:
        copy.wait()


def join(cot_mine, returned, *refs):
    outs, (staged, sems) = refs[:-2], refs[-2:]
    o = outs[0].shape[0]
    stores = []
    for k, out in enumerate(outs):
        rows = slice(k * o, (k + 1) * o)
        staged[k] = (cot_mine[rows, :] + returned[rows, :].astype(F32)).astype(BF16)
        stores.append(pltpu.make_async_copy(staged.at[k], out, sems.at[k]))
        stores[-1].start()
    for copy in stores:
        copy.wait()


def total(position, parts, keep, send):
    core = position[0]
    rows = keep.shape[0]
    for out, c in ((send, 1 - core), (keep, core)):
        start = pl.multiple_of(c * rows, rows)
        acc = parts[0, pl.ds(start, rows), :].astype(F32)
        for s in range(1, parts.shape[0]):
            acc += parts[s, pl.ds(start, rows), :].astype(F32)
        out[...] = -acc


def place(position, keep, received, out):
    core = position[0]
    n = out.shape[1]
    for h in range(2):
        out[2 * h + core] = keep[:, h * n : (h + 1) * n].T
        out[2 * h + 1 - core] = received[:, h * n : (h + 1) * n].T


def shards(green, vectors, weight):
    zs = lax.axis_size("z")
    plane = lax.axis_size("xl") * lax.axis_size("y") * lax.axis_size("xh")
    _, o, m = green.shape
    position = jnp.stack([lax.axis_index("core"), lax.axis_index("xh")]).astype(jnp.int32)

    shape = jax.ShapeDtypeStruct
    dma = pltpu.SemaphoreType.DMA
    payload, spread = call(
        prepare,
        (pltpu.HBM((o + EXTRA, m), BF16), pltpu.HBM((plane, o, m), BF16)),
        [SMEM, SMEM, HBM, HBM],
        "prepare",
        8,
        scratch=[pltpu.VMEM((o, m), BF16), pltpu.VMEM((o + EXTRA, m), BF16), dma((2 + plane,))],
        out_specs=(HBM, HBM),
    )(position, weight, hold(green), hold(vectors))
    held = lax.all_to_all(spread, PLANE, 0, 0, tiled=True).reshape(plane * o, m)

    blocks = gather_line(payload)
    mine = [jnp.stack([blocks[k] for k in group]) for group in (EARLY, LATE)]
    theirs = [shift(group, "core", 1) for group in mine]

    pair_flops = 2 * o * o * m
    exch_mine, exch_theirs, scaled, cot_mine, cot_theirs = call(
        exchange,
        (
            pltpu.VMEM((zs * o, plane * o), BF16),
            pltpu.VMEM((zs * o, plane * o), BF16),
            pltpu.VMEM((zs, m, 2 * o), BF16),
            pltpu.VMEM((zs * o, m), F32),
            pltpu.HBM((zs * o, m), BF16),
        ),
        [VMEM] + [HBM] * 4,
        "exchange",
        24,
        flops=4 * zs * plane * pair_flops,
        scratch=[
            pltpu.VMEM((4, zs // 2, o + EXTRA, m), BF16),
            pltpu.VMEM((zs * o, m), BF16),
            dma((6,)),
        ],
        out_specs=(VMEM,) * 4 + (HBM,),
    )(held, *(hold(x) for x in (*mine, *theirs)))
    returned = shift(cot_theirs, "core", 1)

    grad = call(
        gradient,
        pltpu.HBM((plane, m // 2, 2 * o), BF16),
        [VMEM] * 3,
        "gradient",
        24,
        flops=2 * zs * plane * pair_flops,
        scratch=[pltpu.VMEM((plane, m // 2, 2 * o), BF16), dma((4,))],
        out_specs=HBM,
    )(exch_mine, exch_theirs, scaled)

    sums = call(
        join,
        tuple(pltpu.HBM((o, m), BF16) for _ in range(zs)),
        [VMEM] * 2,
        "join",
        16,
        scratch=[pltpu.VMEM((zs, o, m), BF16), dma((zs,))],
        out_specs=(HBM,) * zs,
    )(cot_mine, returned)
    grad, *sums = lax.optimization_barrier((grad, *sums))
    grad = lax.all_to_all(grad, PLANE, 0, 0, tiled=True)
    cot = None
    for k, block in sorted(zip(EARLY + LATE, sums), key=lambda kb: -min(kb[0], zs - kb[0])):
        part = (block if k == 0 else shift(block, "z", -k)).astype(F32)
        cot = part if cot is None else cot + part
    green_cot = (-weight[0] * cot)[None]

    keep, send = call(total, (shape((m // 4, 2 * o), F32),) * 2, [SMEM, VMEM], "total", 16)(position, grad)
    chol_grad = call(place, shape((4, o, m // 4), F32), [SMEM, VMEM, VMEM], "place", 16)(
        position, keep, shift(send, "core", 1)
    )
    return green_cot, chol_grad


def solution(mesh):
    grid = Mesh(mesh.devices.reshape(2, 8, 4, 2, 2), AXES)
    chol, walk = ("xl", "z", "y"), ("xh", "core")
    every = chol + walk
    return jax.shard_map(
        shards,
        mesh=grid,
        in_specs=(P(every, None, None), P(chol, None, None), P(every)),
        out_specs=(P(every, None, None), P(chol, None, walk)),
        check_vma=False,
    )
```

```python
import jax
import jax.numpy as jnp
from jax import lax
from jax.experimental import pallas as pl
from jax.experimental.pallas import tpu as pltpu
from jax.sharding import Mesh, PartitionSpec as P


F32 = jnp.float32
BF16 = jnp.bfloat16
AXES = ("xl", "z", "y", "xh", "core")
PLANE = ("xl", "y", "xh")
VMEM = pl.BlockSpec(memory_space=pltpu.VMEM)
HBM = pl.BlockSpec(memory_space=pltpu.HBM)
SMEM = pl.BlockSpec(memory_space=pltpu.SMEM)
EXTRA = 16
MINE = ((0, 0), (1, 0), (1, 2), (2, 0), (2, 2), (3, 1), (3, 3), (4, 1))
THEIRS = ((0, 1), (3, 0), (3, 2), (4, 0), (4, 2), (1, 1), (1, 3), (2, 1))
OFFSETS = (0, 1, 2, 3, 4, -1, -2, -3)


def opposed(block, axis, distance):
    if axis == "x":
        n = lax.axis_size("xl") * lax.axis_size("xh")
        flat = [(x % 2) * (n // 2) + x // 2 for x in range(n)]
        names = ("xl", "xh", "core")
    else:
        n = lax.axis_size(axis)
        flat = list(range(n))
        names = (axis, "core")
    route = []
    for i in range(n):
        route.append((2 * flat[i], 2 * flat[(i + distance) % n]))
        route.append((2 * flat[i] + 1, 2 * flat[(i - distance) % n] + 1))
    return lax.ppermute(block, names, route)


def swap(block):
    return lax.ppermute(block, "core", [(0, 1), (1, 0)])


def hold(x):
    return pltpu.with_memory_space_constraint(x, pltpu.HBM)


def call(body, outs, ins, mib, flops=0, moved=2 << 20, scratch=(), out_specs=None):
    return pl.pallas_call(
        body,
        out_shape=outs,
        in_specs=ins,
        out_specs=jax.tree.map(lambda _: VMEM, outs) if out_specs is None else out_specs,
        scratch_shapes=scratch,
        compiler_params=pltpu.CompilerParams(vmem_limit_bytes=mib << 20),
        cost_estimate=pl.CostEstimate(flops=flops, bytes_accessed=moved, transcendentals=0),
    )


def prepare(position, weight, green, vectors, payload, ordered, sems):
    core = position[0]
    o, m = green.shape[1:]
    copies = [pltpu.make_async_copy(green, payload.at[:, pl.ds(0, o)], sems.at[4])]
    for k, v in enumerate((core, core + 2, 1 - core, 3 - core)):
        copies.append(pltpu.make_async_copy(vectors.at[v], ordered.at[k], sems.at[k]))
    for copy in copies:
        copy.start()
    w = jnp.full((EXTRA, m), weight[0], F32)
    high = w.astype(BF16).astype(F32)
    middle = (w - high).astype(BF16).astype(F32)
    low = w - high - middle
    row = lax.broadcasted_iota(jnp.int32, w.shape, 0)
    tile = jnp.where(row == 0, high, jnp.where(row == 1, middle, jnp.where(row == 2, low, 0.0)))
    payload[0, o:, :] = tile.astype(BF16)
    for copy in copies:
        copy.wait()


def collect(groups, vectors):
    o, _ = groups[0].shape[1:]
    for g, group in enumerate(groups):
        for j in range(2):
            vectors[(2 * g + j) * o : (2 * g + j + 1) * o, :] = group[j]


def multiply(vectors, walkers, exch, scaled=None):
    o = walkers[0].shape[1] - EXTRA
    count = vectors.shape[0] // o
    quad = 4
    places = MINE + THEIRS
    for i in range(len(places) // 2):
        pair = places[2 * i : 2 * i + 2]
        blocks = [walkers[a][k, :o, :] for a, k in pair]
        both = jnp.concatenate(blocks)
        for q in range(count // quad):
            part = lax.dot_general(
                vectors[q * quad * o : (q + 1) * quad * o, :],
                both,
                (((1,), (1,)), ((), ())),
                preferred_element_type=F32,
            ).astype(BF16)
            for g in range(quad):
                for w in range(2):
                    exch[
                        (2 * i + w) * o : (2 * i + w + 1) * o, (q * quad + g) * o : (q * quad + g + 1) * o
                    ] = part[g * o : (g + 1) * o, w * o : (w + 1) * o]
        if scaled is not None:
            for w, (a, k) in enumerate(pair):
                weight = jnp.sum(walkers[a][k, o:, :].astype(F32), axis=0, keepdims=True)
                scaled[i, :, w * o : (w + 1) * o] = (blocks[w].astype(F32) * weight).astype(BF16).T


def reduce_walkers(scaled, exch, store):
    pairs, m, two = scaled.shape
    width = 2 * two
    for c in range(exch.shape[1] // width):
        acc = jnp.zeros((m, width), F32)
        for i in range(pairs):
            acc += jnp.dot(
                scaled[i], exch[i * two : (i + 1) * two, c * width : (c + 1) * width], preferred_element_type=F32
            )
        acc = acc.astype(BF16)
        for s in range(width // two):
            for h in range(2):
                store(c * (width // two) + s, h, acc[h * m // 2 : (h + 1) * m // 2, s * two : (s + 1) * two])


def first(chip, near, rest, w1, w2, v0, v1, v2, v3, exch, scaled, vectors, grad):
    collect((v0, v1, v2, v3), vectors)
    multiply(vectors, (chip, near, rest, w1, w2), exch, scaled)

    def store(group, h, block):
        grad[2 * group + h] = block

    reduce_walkers(scaled, exch, store)


def second(chip, near, rest, w1, w2, v0, v1, v2, v3, exch0, vectors0, exch, cot_mine, cot_theirs, vectors, cot, sems):
    collect((v0, v1, v2, v3), vectors)
    multiply(vectors, (chip, near, rest, w1, w2), exch)
    half = cot_mine.shape[0]
    run = 512
    stores = []
    for r in range(2 * half // run):
        base = (half + r * run) % (2 * half)
        rows = slice(base, base + run)
        part = jnp.dot(exch0[rows, :], vectors0[...], preferred_element_type=F32)
        part += jnp.dot(exch[rows, :], vectors[...], preferred_element_type=F32)
        if base >= half:
            target = slice(base - half, base - half + run)
            cot[target, :] = part.astype(BF16)
            stores.append(pltpu.make_async_copy(cot.at[target], cot_theirs.at[target], sems.at[r]))
            stores[-1].start()
        else:
            cot_mine[rows, :] = part
    for copy in stores:
        copy.wait()


def gradient(position, scaled, exch, grad0, grad, staged, sems):
    core, column, y, rows = position[0], position[1], position[2], position[3]
    step = 2 * core - 1
    places = [lax.rem(y + d + rows, rows) for d in (0, step, 2, -step)]
    copies = []
    for g, place in enumerate(places):
        target = grad.at[pl.ds((column * rows + place) * 2, 2)]
        copies.append(pltpu.make_async_copy(grad0.at[pl.ds(2 * g, 2)], target, sems.at[g]))
        copies[-1].start()

    def store(group, h, block):
        staged[2 * group + h] = block
        if h == 1:
            target = grad.at[pl.ds(((1 - column) * rows + places[group]) * 2, 2)]
            copies.append(pltpu.make_async_copy(staged.at[pl.ds(2 * group, 2)], target, sems.at[4 + group]))
            copies[-1].start()

    reduce_walkers(scaled, exch, store)
    for copy in copies:
        copy.wait()


def join(cot_mine, returned, *refs):
    outs, (staged, sems) = refs[:-2], refs[-2:]
    o = outs[0].shape[0]
    stores = []
    for k, out in enumerate(outs):
        rows = slice(k * o, (k + 1) * o)
        staged[k] = (cot_mine[rows, :] + returned[rows, :].astype(F32)).astype(BF16)
        stores.append(pltpu.make_async_copy(staged.at[k], out, sems.at[k]))
        stores[-1].start()
    for copy in stores:
        copy.wait()


def total(position, parts, keep, send):
    core = position[0]
    rows = keep.shape[0]
    for out, c in ((send, 1 - core), (keep, core)):
        start = pl.multiple_of(c * rows, rows)
        acc = parts[0, pl.ds(start, rows), :].astype(F32)
        for s in range(1, parts.shape[0]):
            acc += parts[s, pl.ds(start, rows), :].astype(F32)
        out[...] = -acc


def place(position, keep, received, out):
    core = position[0]
    n = out.shape[1]
    for h in range(2):
        out[2 * h + core] = keep[:, h * n : (h + 1) * n].T
        out[2 * h + 1 - core] = received[:, h * n : (h + 1) * n].T


def step(green, vectors, weight):
    zs, ys = lax.axis_size("z"), lax.axis_size("y")
    plane = lax.axis_size("xl") * ys * lax.axis_size("xh")
    _, o, m = green.shape
    index = [lax.axis_index(a) for a in ("core", "xl", "y")]
    position = jnp.stack([*index, jnp.int32(ys)]).astype(jnp.int32)
    shape = jax.ShapeDtypeStruct
    dma = pltpu.SemaphoreType.DMA

    payload, ordered = call(
        prepare,
        (pltpu.VMEM((1, o + EXTRA, m), BF16), pltpu.VMEM((4, o, m), BF16)),
        [SMEM, SMEM, HBM, HBM],
        8,
        scratch=[dma((5,))],
    )(position, weight, hold(green), hold(vectors))

    y1 = opposed(ordered, "y", 1)
    chip = jnp.concatenate([payload, swap(payload)])
    z2 = opposed(chip, "z", 2)
    z1 = opposed(chip, "z", 1)
    x0 = opposed(ordered[:2], "x", 1)
    y2 = opposed(y1[:2], "y", 1)
    x1 = opposed(y1, "x", 1)
    y3 = swap(y1[2:])
    z3 = opposed(z2, "z", 1)
    z4 = opposed(z2[:1], "z", 2)
    near = jnp.concatenate([z1, z2])
    w1 = swap(near)
    x2 = opposed(y2, "x", 1)
    x3 = swap(x1[2:])
    rest = jnp.concatenate([z3, z4])
    w2 = swap(rest)

    half = plane // 2
    pair_flops = 2 * o * o * m
    exch0, scaled, vectors0, grad0 = call(
        first,
        (
            pltpu.VMEM((2 * zs * o, half * o), BF16),
            pltpu.VMEM((zs, m, 2 * o), BF16),
            pltpu.VMEM((half * o, m), BF16),
            pltpu.VMEM((half, m // 2, 2 * o), BF16),
        ),
        [VMEM] * 9,
        24,
        flops=2 * zs * plane * pair_flops,
    )(chip, near, rest, w1, w2, ordered, y1, y2, y3)

    exch1, cot_mine, cot_theirs = call(
        second,
        (pltpu.VMEM((2 * zs * o, half * o), BF16), pltpu.VMEM((zs * o, m), F32), pltpu.HBM((zs * o, m), BF16)),
        [VMEM] * 11,
        32,
        flops=3 * zs * plane * pair_flops,
        scratch=[pltpu.VMEM((half * o, m), BF16), pltpu.VMEM((zs * o, m), BF16), dma((4,))],
        out_specs=(VMEM, VMEM, HBM),
    )(chip, near, rest, w1, w2, x0, x1, x2, x3, exch0, vectors0)
    returned = swap(cot_theirs)

    grad = call(
        gradient,
        pltpu.HBM((plane, m // 2, 2 * o), BF16),
        [SMEM, VMEM, VMEM, VMEM],
        24,
        flops=zs * plane * pair_flops,
        scratch=[pltpu.VMEM((half, m // 2, 2 * o), BF16), dma((8,))],
        out_specs=HBM,
    )(position, scaled, exch1, grad0)

    sums = call(
        join,
        tuple(pltpu.HBM((o, m), BF16) for _ in range(zs)),
        [VMEM] * 2,
        16,
        scratch=[pltpu.VMEM((zs, o, m), BF16), dma((zs,))],
        out_specs=(HBM,) * zs,
    )(cot_mine, returned)
    grad, *sums = lax.optimization_barrier((grad, *sums))
    grad = lax.all_to_all(grad, PLANE, 0, 0, tiled=True)
    cot = None
    for k, block in sorted(zip(OFFSETS, sums), key=lambda kb: -abs(kb[0])):
        part = (block if k == 0 else opposed(block, "z", -k)).astype(F32)
        cot = part if cot is None else cot + part
    green_cot = (-weight[0] * cot)[None]

    keep, send = call(total, (shape((m // 4, 2 * o), F32),) * 2, [SMEM, VMEM], 16)(position, grad)
    chol_grad = call(place, shape((4, o, m // 4), F32), [SMEM, VMEM, VMEM], 16)(position, keep, swap(send))
    return green_cot, chol_grad


def solution(mesh):
    grid = Mesh(mesh.devices.reshape(2, 8, 4, 2, 2), AXES)
    chol, walk = ("xl", "z", "y"), ("xh", "core")
    every = chol + walk
    return jax.shard_map(
        step,
        mesh=grid,
        in_specs=(P(every, None, None), P(chol, None, None), P(every)),
        out_specs=(P(every, None, None), P(chol, None, walk)),
        check_vma=False,
    )
```

```python
import jax
import jax.numpy as jnp
from jax import lax
from jax.experimental import pallas as pl
from jax.experimental.pallas import tpu as pltpu
from jax.sharding import Mesh, PartitionSpec as P


F32 = jnp.float32
BF16 = jnp.bfloat16
AXES = ("xl", "z", "y", "xh", "core")
PLANE = ("xl", "y", "xh")
VMEM = pl.BlockSpec(memory_space=pltpu.VMEM)
HBM = pl.BlockSpec(memory_space=pltpu.HBM)
SMEM = pl.BlockSpec(memory_space=pltpu.SMEM)
EXTRA = 16
EARLY_MINE = ((0, 0), (1, 0), (1, 2), (3, 1), (3, 3))
EARLY_THEIRS = ((0, 1), (3, 0), (3, 2), (1, 1), (1, 3))
LATE_MINE = ((2, 0), (2, 2), (4, 1))
LATE_THEIRS = ((4, 0), (4, 2), (2, 1))
OFFSETS = (0, 1, 2, -1, -2, 3, 4, -3)


def opposed(block, axis, distance):
    if axis == "x":
        n = lax.axis_size("xl") * lax.axis_size("xh")
        flat = [(x % 2) * (n // 2) + x // 2 for x in range(n)]
        names = ("xl", "xh", "core")
    else:
        n = lax.axis_size(axis)
        flat = list(range(n))
        names = (axis, "core")
    route = []
    for i in range(n):
        route.append((2 * flat[i], 2 * flat[(i + distance) % n]))
        route.append((2 * flat[i] + 1, 2 * flat[(i - distance) % n] + 1))
    return lax.ppermute(block, names, route)


def swap(block):
    return lax.ppermute(block, "core", [(0, 1), (1, 0)])


def hold(x):
    return pltpu.with_memory_space_constraint(x, pltpu.HBM)


def call(body, outs, ins, mib, flops=0, moved=2 << 20, scratch=(), out_specs=None):
    return pl.pallas_call(
        body,
        out_shape=outs,
        in_specs=ins,
        out_specs=jax.tree.map(lambda _: VMEM, outs) if out_specs is None else out_specs,
        scratch_shapes=scratch,
        compiler_params=pltpu.CompilerParams(vmem_limit_bytes=mib << 20),
        cost_estimate=pl.CostEstimate(flops=flops, bytes_accessed=moved, transcendentals=0),
    )


def prepare(position, weight, green, vectors, payload, ordered, sems):
    core = position[0]
    o, m = green.shape[1:]
    copies = [pltpu.make_async_copy(green, payload.at[:, pl.ds(0, o)], sems.at[4])]
    for k, v in enumerate((core, core + 2, 1 - core, 3 - core)):
        copies.append(pltpu.make_async_copy(vectors.at[v], ordered.at[k], sems.at[k]))
    for copy in copies:
        copy.start()
    w = jnp.full((EXTRA, m), weight[0], F32)
    high = w.astype(BF16).astype(F32)
    middle = (w - high).astype(BF16).astype(F32)
    low = w - high - middle
    row = lax.broadcasted_iota(jnp.int32, w.shape, 0)
    tile = jnp.where(row == 0, high, jnp.where(row == 1, middle, jnp.where(row == 2, low, 0.0)))
    payload[0, o:, :] = tile.astype(BF16)
    for copy in copies:
        copy.wait()


def collect(groups, vectors):
    o, _ = groups[0].shape[1:]
    for g, group in enumerate(groups):
        for j in range(2):
            vectors[(2 * g + j) * o : (2 * g + j + 1) * o, :] = group[j]


def multiply(vectors, walkers, places, exch, base=0, scaled=None):
    o = vectors.shape[0] // 8
    quad = 4
    for i in range(len(places) // 2):
        pair = places[2 * i : 2 * i + 2]
        blocks = [walkers[a][k, :o, :] for a, k in pair]
        both = jnp.concatenate(blocks)
        for q in range(2):
            part = lax.dot_general(
                vectors[q * quad * o : (q + 1) * quad * o, :],
                both,
                (((1,), (1,)), ((), ())),
                preferred_element_type=F32,
            ).astype(BF16)
            for g in range(quad):
                for w in range(2):
                    row = base + (2 * i + w) * o
                    exch[row : row + o, (q * quad + g) * o : (q * quad + g + 1) * o] = part[
                        g * o : (g + 1) * o, w * o : (w + 1) * o
                    ]
        if scaled is not None:
            for w, (a, k) in enumerate(pair):
                weight = jnp.sum(walkers[a][k, o:, :].astype(F32), axis=0, keepdims=True)
                scaled[i, :, w * o : (w + 1) * o] = (blocks[w].astype(F32) * weight).astype(BF16).T


def reduce_walkers(terms, store):
    scaled, _, exch, _ = terms[0]
    _, m, two = scaled.shape
    width = 2 * two
    for c in range(exch.shape[1] // width):
        acc = jnp.zeros((m, width), F32)
        for scaled, i, exch, row in terms:
            acc += jnp.dot(
                scaled[i], exch[row : row + two, c * width : (c + 1) * width], preferred_element_type=F32
            )
        acc = acc.astype(BF16)
        for s in range(width // two):
            for h in range(2):
                store(c * (width // two) + s, h, acc[h * m // 2 : (h + 1) * m // 2, s * two : (s + 1) * two])


def terms_of(scaled, exch, base=0):
    two = scaled.shape[2]
    return [(scaled, i, exch, base + i * two) for i in range(scaled.shape[0])]


def started(*copies):
    for copy in copies:
        copy.start()
    return list(copies)


def early(chip, near, w1, v0, v1, v2, v3, exch, scaled, vectors, kept_exch, kept_vectors, sems):
    collect((v0, v1, v2, v3), vectors)
    copies = started(pltpu.make_async_copy(vectors, kept_vectors, sems.at[0]))
    multiply(vectors, {0: chip, 1: near, 3: w1}, EARLY_MINE + EARLY_THEIRS, exch, scaled=scaled)
    rows = kept_exch.shape[0]
    copies += started(pltpu.make_async_copy(exch.at[pl.ds(0, rows)], kept_exch, sems.at[1]))
    for copy in copies:
        copy.wait()


def first(rest, w2, exch0, scaled0, vectors, exch, scaled, grad, kept_exch, sems):
    multiply(vectors, {2: rest, 4: w2}, LATE_MINE + LATE_THEIRS, exch, scaled=scaled)
    rows = kept_exch.shape[0]
    copies = started(pltpu.make_async_copy(exch.at[pl.ds(0, rows)], kept_exch, sems.at[0]))

    def store(group, h, block):
        grad[2 * group + h] = block

    reduce_walkers(terms_of(scaled0, exch0) + terms_of(scaled, exch), store)
    for copy in copies:
        copy.wait()


def second(
    chip, near, rest, w1, w2, v0, v1, v2, v3, exch0, exch1, vectors0, exch, cot_theirs, kept_exch, kept_vectors, vectors, cot, sems
):
    o = vectors.shape[0] // 8
    collect((v0, v1, v2, v3), vectors)
    places = EARLY_MINE + EARLY_THEIRS + LATE_MINE + LATE_THEIRS
    multiply(vectors, (chip, near, rest, w1, w2), places, exch)
    split, total_early = len(EARLY_MINE) * o, 2 * len(EARLY_MINE) * o
    count = len(LATE_MINE) * o
    copies = started(
        pltpu.make_async_copy(vectors, kept_vectors, sems.at[0]),
        pltpu.make_async_copy(exch.at[pl.ds(0, split)], kept_exch.at[pl.ds(0, split)], sems.at[1]),
        pltpu.make_async_copy(exch.at[pl.ds(total_early, count)], kept_exch.at[pl.ds(split, count)], sems.at[2]),
    )
    for r, (own, row, size, base) in enumerate(((exch0, split, split, 0), (exch1, count, count, total_early))):
        target = slice(r * split, r * split + size)
        part = jnp.dot(own[row : row + size, :], vectors0[...], preferred_element_type=F32)
        part += jnp.dot(exch[base + row : base + row + size, :], vectors[...], preferred_element_type=F32)
        cot[target, :] = part.astype(BF16)
        copies += started(pltpu.make_async_copy(cot.at[target], cot_theirs.at[target], sems.at[3 + r]))
    for copy in copies:
        copy.wait()


def gradient(position, scaled0, scaled1, exch, grad0, grad, staged, sems):
    core, column, y, rows = position[0], position[1], position[2], position[3]
    step = 2 * core - 1
    places = [lax.rem(y + d + rows, rows) for d in (0, step, 2, -step)]
    copies = []
    for g, place in enumerate(places):
        target = grad.at[pl.ds((column * rows + place) * 2, 2)]
        copies += started(pltpu.make_async_copy(grad0.at[pl.ds(2 * g, 2)], target, sems.at[g]))

    def store(group, h, block):
        staged[2 * group + h] = block
        if h == 1:
            target = grad.at[pl.ds(((1 - column) * rows + places[group]) * 2, 2)]
            copies.extend(started(pltpu.make_async_copy(staged.at[pl.ds(2 * group, 2)], target, sems.at[4 + group])))

    base = scaled0.shape[0] * scaled0.shape[2]
    reduce_walkers(terms_of(scaled0, exch) + terms_of(scaled1, exch, base), store)
    for copy in copies:
        copy.wait()


def finish(kept_early, kept_late, vectors0, kept1, vectors1, returned, *refs):
    outs, (exch, vectors, staged, sems, out_sems) = refs[:-5], refs[-5:]
    o = outs[0].shape[0]
    early_rows = kept_early.shape[0]
    cuts = [0, 2 * o, 4 * o, 6 * o, 8 * o]
    pieces = []
    for lo, hi in zip(cuts, cuts[1:]):
        piece = []
        for source, at, a, b in (
            (kept_early, 0, lo, min(hi, early_rows)),
            (kept_late, early_rows, max(lo, early_rows), hi),
        ):
            if a < b:
                k = len(pieces) * 3 + len(piece)
                piece.append(
                    pltpu.make_async_copy(
                        source.at[pl.ds(a - at, b - a)], exch.at[0, pl.ds(a, b - a)], sems.at[2 + k]
                    )
                )
        k = len(pieces) * 3 + 2
        other = pltpu.make_async_copy(kept1.at[pl.ds(lo, hi - lo)], exch.at[1, pl.ds(lo, hi - lo)], sems.at[2 + k])
        pieces.append((piece, other))
    load0 = started(pltpu.make_async_copy(vectors0, vectors.at[0], sems.at[0]))[0]
    started(*pieces[0][0])
    load1 = started(pltpu.make_async_copy(vectors1, vectors.at[1], sems.at[1]))[0]
    pieces[0][1].start()
    for piece, other in pieces[1:]:
        started(*piece, other)
    load0.wait()
    stores = []
    for r, (piece, other) in enumerate(pieces):
        lo, hi = cuts[r], cuts[r + 1]
        for copy in piece:
            copy.wait()
        part = jnp.dot(exch[0, lo:hi, :], vectors[0], preferred_element_type=F32)
        if r == 0:
            load1.wait()
        other.wait()
        part += jnp.dot(exch[1, lo:hi, :], vectors[1], preferred_element_type=F32)
        part += returned[lo:hi, :].astype(F32)
        for w in range((hi - lo) // o):
            k = lo // o + w
            staged[k] = part[w * o : (w + 1) * o, :].astype(BF16)
            stores += started(pltpu.make_async_copy(staged.at[k], outs[k], out_sems.at[k]))
    for copy in stores:
        copy.wait()


def total(position, parts, keep, send):
    core = position[0]
    rows = keep.shape[0]
    for out, c in ((send, 1 - core), (keep, core)):
        start = pl.multiple_of(c * rows, rows)
        acc = parts[0, pl.ds(start, rows), :].astype(F32)
        for s in range(1, parts.shape[0]):
            acc += parts[s, pl.ds(start, rows), :].astype(F32)
        out[...] = -acc


def place(position, keep, received, out):
    core = position[0]
    n = out.shape[1]
    for h in range(2):
        out[2 * h + core] = keep[:, h * n : (h + 1) * n].T
        out[2 * h + 1 - core] = received[:, h * n : (h + 1) * n].T


def step(green, vectors, weight):
    zs, ys = lax.axis_size("z"), lax.axis_size("y")
    plane = lax.axis_size("xl") * ys * lax.axis_size("xh")
    _, o, m = green.shape
    index = [lax.axis_index(a) for a in ("core", "xl", "y")]
    position = jnp.stack([*index, jnp.int32(ys)]).astype(jnp.int32)
    shape = jax.ShapeDtypeStruct
    dma = pltpu.SemaphoreType.DMA

    payload, ordered = call(
        prepare,
        (pltpu.VMEM((1, o + EXTRA, m), BF16), pltpu.VMEM((4, o, m), BF16)),
        [SMEM, SMEM, HBM, HBM],
        8,
        scratch=[dma((5,))],
    )(position, weight, hold(green), hold(vectors))

    y1 = opposed(ordered, "y", 1)
    chip = jnp.concatenate([payload, swap(payload)])
    z2 = opposed(chip, "z", 2)
    z1 = opposed(chip, "z", 1)
    x0 = opposed(ordered[:2], "x", 1)
    y2 = opposed(y1[:2], "y", 1)
    x1 = opposed(y1, "x", 1)
    y3 = swap(y1[2:])
    z3 = opposed(z2, "z", 1)
    z4 = opposed(z2[:1], "z", 2)
    near = jnp.concatenate([z1, z2])
    w1 = swap(near)
    x2 = opposed(y2, "x", 1)
    x3 = swap(x1[2:])
    rest = jnp.concatenate([z3, z4])
    w2 = swap(rest)

    half = plane // 2
    pair_flops = 2 * o * o * m
    ne, nl = len(EARLY_MINE), len(LATE_MINE)
    exch0, scaled0, vectors0, kept_early, kept_vectors0 = call(
        early,
        (
            pltpu.VMEM((2 * ne * o, half * o), BF16),
            pltpu.VMEM((ne, m, 2 * o), BF16),
            pltpu.VMEM((half * o, m), BF16),
            pltpu.HBM((ne * o, half * o), BF16),
            pltpu.HBM((half * o, m), BF16),
        ),
        [VMEM] * 7,
        20,
        flops=2 * ne * half * pair_flops,
        scratch=[dma((2,))],
        out_specs=(VMEM,) * 3 + (HBM,) * 2,
    )(chip, near, w1, ordered, y1, y2, y3)

    exch1, scaled1, grad0, kept_late = call(
        first,
        (
            pltpu.VMEM((2 * nl * o, half * o), BF16),
            pltpu.VMEM((nl, m, 2 * o), BF16),
            pltpu.VMEM((half, m // 2, 2 * o), BF16),
            pltpu.HBM((nl * o, half * o), BF16),
        ),
        [VMEM] * 5,
        24,
        flops=2 * zs * plane * pair_flops,
        scratch=[dma((1,))],
        out_specs=(VMEM,) * 3 + (HBM,),
    )(rest, w2, exch0, scaled0, vectors0)

    exch, cot_theirs, kept1, kept_vectors1 = call(
        second,
        (
            pltpu.VMEM((2 * zs * o, half * o), BF16),
            pltpu.HBM((zs * o, m), BF16),
            pltpu.HBM((zs * o, half * o), BF16),
            pltpu.HBM((half * o, m), BF16),
        ),
        [VMEM] * 12,
        32,
        flops=2 * zs * plane * pair_flops,
        scratch=[pltpu.VMEM((half * o, m), BF16), pltpu.VMEM((zs * o, m), BF16), dma((5,))],
        out_specs=(VMEM,) + (HBM,) * 3,
    )(chip, near, rest, w1, w2, x0, x1, x2, x3, exch0, exch1, vectors0)
    returned = swap(cot_theirs)

    grad = call(
        gradient,
        pltpu.HBM((plane, m // 2, 2 * o), BF16),
        [SMEM] + [VMEM] * 4,
        24,
        flops=zs * plane * pair_flops,
        scratch=[pltpu.VMEM((half, m // 2, 2 * o), BF16), dma((8,))],
        out_specs=HBM,
    )(position, scaled0, scaled1, exch, grad0)

    grad = lax.all_to_all(grad, PLANE, 0, 0, tiled=True)
    sums = call(
        finish,
        tuple(pltpu.HBM((o, m), BF16) for _ in range(zs)),
        [HBM] * 5 + [VMEM],
        24,
        flops=zs * plane * pair_flops,
        scratch=[
            pltpu.VMEM((2, zs * o, half * o), BF16),
            pltpu.VMEM((2, half * o, m), BF16),
            pltpu.VMEM((zs, o, m), BF16),
            dma((14,)),
            dma((zs,)),
        ],
        out_specs=(HBM,) * zs,
    )(*(hold(x) for x in (kept_early, kept_late, kept_vectors0, kept1, kept_vectors1)), returned)
    cot = None
    for k, block in sorted(zip(OFFSETS, sums), key=lambda kb: -abs(kb[0])):
        part = (block if k == 0 else opposed(block, "z", -k)).astype(F32)
        cot = part if cot is None else cot + part
    minus = -weight[0]
    green_cot = (minus * cot)[None]

    keep, send = call(total, (shape((m // 4, 2 * o), F32),) * 2, [SMEM, VMEM], 16)(position, grad)
    chol_grad = call(place, shape((4, o, m // 4), F32), [SMEM, VMEM, VMEM], 16)(position, keep, swap(send))
    return green_cot, chol_grad


def solution(mesh):
    grid = Mesh(mesh.devices.reshape(2, 8, 4, 2, 2), AXES)
    chol, walk = ("xl", "z", "y"), ("xh", "core")
    every = chol + walk
    return jax.shard_map(
        step,
        mesh=grid,
        in_specs=(P(every, None, None), P(chol, None, None), P(every)),
        out_specs=(P(every, None, None), P(chol, None, walk)),
        check_vma=False,
    )
```

```python
import jax
import jax.numpy as jnp
from jax import lax
from jax.experimental import pallas as pl
from jax.experimental.pallas import tpu as pltpu
from jax.sharding import Mesh, PartitionSpec as P


F32 = jnp.float32
BF16 = jnp.bfloat16
AXES = ("xl", "z", "y", "xh", "core")
PLANE = ("xl", "y", "xh")
VMEM = pl.BlockSpec(memory_space=pltpu.VMEM)
HBM = pl.BlockSpec(memory_space=pltpu.HBM)
SMEM = pl.BlockSpec(memory_space=pltpu.SMEM)
EXTRA = 16
EARLY_MINE = ((0, 0), (1, 0), (1, 2), (3, 1), (3, 3))
EARLY_THEIRS = ((0, 1), (3, 0), (3, 2), (1, 1), (1, 3))
LATE_MINE = ((2, 0), (2, 2), (4, 1))
LATE_THEIRS = ((4, 0), (4, 2), (2, 1))
OFFSETS = (0, 1, 2, -1, -2, 3, 4, -3)


def opposed(block, axis, distance):
    if axis == "x":
        n = lax.axis_size("xl") * lax.axis_size("xh")
        flat = [(x % 2) * (n // 2) + x // 2 for x in range(n)]
        names = ("xl", "xh", "core")
    else:
        n = lax.axis_size(axis)
        flat = list(range(n))
        names = (axis, "core")
    route = []
    for i in range(n):
        route.append((2 * flat[i], 2 * flat[(i + distance) % n]))
        route.append((2 * flat[i] + 1, 2 * flat[(i - distance) % n] + 1))
    return lax.ppermute(block, names, route)


def swap(block):
    return lax.ppermute(block, "core", [(0, 1), (1, 0)])


def hold(x):
    return pltpu.with_memory_space_constraint(x, pltpu.HBM)


def call(body, outs, ins, mib, flops=0, moved=2 << 20, scratch=(), out_specs=None):
    return pl.pallas_call(
        body,
        out_shape=outs,
        in_specs=ins,
        out_specs=jax.tree.map(lambda _: VMEM, outs) if out_specs is None else out_specs,
        scratch_shapes=scratch,
        compiler_params=pltpu.CompilerParams(vmem_limit_bytes=mib << 20),
        cost_estimate=pl.CostEstimate(flops=flops, bytes_accessed=moved, transcendentals=0),
    )


def prepare(position, weight, green, vectors, payload, ordered, sems):
    core = position[0]
    o, m = green.shape[1:]
    copies = [pltpu.make_async_copy(green, payload.at[:, pl.ds(0, o)], sems.at[4])]
    for k, v in enumerate((core, core + 2, 1 - core, 3 - core)):
        copies.append(pltpu.make_async_copy(vectors.at[v], ordered.at[k], sems.at[k]))
    for copy in copies:
        copy.start()
    w = jnp.full((EXTRA, m), weight[0], F32)
    high = w.astype(BF16).astype(F32)
    middle = (w - high).astype(BF16).astype(F32)
    low = w - high - middle
    row = lax.broadcasted_iota(jnp.int32, w.shape, 0)
    tile = jnp.where(row == 0, high, jnp.where(row == 1, middle, jnp.where(row == 2, low, 0.0)))
    payload[0, o:, :] = tile.astype(BF16)
    for copy in copies:
        copy.wait()


def collect(groups, vectors):
    o, _ = groups[0].shape[1:]
    for g, group in enumerate(groups):
        for j in range(2):
            vectors[(2 * g + j) * o : (2 * g + j + 1) * o, :] = group[j]


def multiply(vectors, walkers, places, exch, base=0, scaled=None):
    o = vectors.shape[0] // 8
    quad = 4
    for i in range(len(places) // 2):
        pair = places[2 * i : 2 * i + 2]
        blocks = [walkers[a][k, :o, :] for a, k in pair]
        both = jnp.concatenate(blocks)
        for q in range(2):
            part = lax.dot_general(
                vectors[q * quad * o : (q + 1) * quad * o, :],
                both,
                (((1,), (1,)), ((), ())),
                preferred_element_type=F32,
            ).astype(BF16)
            for g in range(quad):
                for w in range(2):
                    row = base + (2 * i + w) * o
                    exch[row : row + o, (q * quad + g) * o : (q * quad + g + 1) * o] = part[
                        g * o : (g + 1) * o, w * o : (w + 1) * o
                    ]
        if scaled is not None:
            for w, (a, k) in enumerate(pair):
                weight = jnp.sum(walkers[a][k, o:, :].astype(F32), axis=0, keepdims=True)
                scaled[i, :, w * o : (w + 1) * o] = (blocks[w].astype(F32) * weight).astype(BF16).T


def reduce_walkers(terms, store):
    scaled, _, exch, _ = terms[0]
    _, m, two = scaled.shape
    width = two
    for c in range(exch.shape[1] // width):
        acc = jnp.zeros((m, width), F32)
        for scaled, i, exch, row in terms:
            acc += jnp.dot(
                scaled[i], exch[row : row + two, c * width : (c + 1) * width], preferred_element_type=F32
            )
        acc = acc.astype(BF16)
        for s in range(width // two):
            for h in range(2):
                store(c * (width // two) + s, h, acc[h * m // 2 : (h + 1) * m // 2, s * two : (s + 1) * two])


def terms_of(scaled, exch):
    two = scaled.shape[2]
    return [(scaled, i, exch, i * two) for i in range(scaled.shape[0])]


def started(*copies):
    for copy in copies:
        copy.start()
    return list(copies)


def early(chip, near, w1, v0, v1, v2, v3, exch, scaled, vectors, kept_exch, kept_vectors, sems):
    collect((v0, v1, v2, v3), vectors)
    copies = started(pltpu.make_async_copy(vectors, kept_vectors, sems.at[0]))
    multiply(vectors, {0: chip, 1: near, 3: w1}, EARLY_MINE + EARLY_THEIRS, exch, scaled=scaled)
    rows = kept_exch.shape[0]
    copies += started(pltpu.make_async_copy(exch.at[pl.ds(0, rows)], kept_exch, sems.at[1]))
    for copy in copies:
        copy.wait()


def first(rest, w2, exch0, scaled0, vectors, exch, scaled, grad, kept_exch, sems):
    multiply(vectors, {2: rest, 4: w2}, LATE_MINE + LATE_THEIRS, exch, scaled=scaled)
    rows = kept_exch.shape[0]
    copies = started(pltpu.make_async_copy(exch.at[pl.ds(0, rows)], kept_exch, sems.at[0]))

    def store(group, h, block):
        grad[2 * group + h] = block

    reduce_walkers(terms_of(scaled0, exch0) + terms_of(scaled, exch), store)
    for copy in copies:
        copy.wait()


def beyond(chip, near, w1, v0, v1, v2, v3, exch, vectors, kept_exch, kept_vectors, sems):
    collect((v0, v1, v2, v3), vectors)
    copies = started(pltpu.make_async_copy(vectors, kept_vectors, sems.at[0]))
    multiply(vectors, {0: chip, 1: near, 3: w1}, EARLY_MINE + EARLY_THEIRS, exch)
    rows = kept_exch.shape[0]
    copies += started(pltpu.make_async_copy(exch.at[pl.ds(0, rows)], kept_exch, sems.at[1]))
    for copy in copies:
        copy.wait()


def second(rest, w2, exch0, exch1, exch2, vectors0, vectors1, exch, cot_theirs, kept_exch, cot, sems):
    multiply(vectors1, {2: rest, 4: w2}, LATE_MINE + LATE_THEIRS, exch)
    split, count = exch0.shape[0] // 2, exch1.shape[0] // 2
    copies = started(pltpu.make_async_copy(exch.at[pl.ds(0, count)], kept_exch, sems.at[0]))
    for r, (own, other, size) in enumerate(((exch0, exch2, split), (exch1, exch, count))):
        target = slice(r * split, r * split + size)
        part = jnp.dot(own[size : 2 * size, :], vectors0[...], preferred_element_type=F32)
        part += jnp.dot(other[size : 2 * size, :], vectors1[...], preferred_element_type=F32)
        cot[target, :] = part.astype(BF16)
        copies += started(pltpu.make_async_copy(cot.at[target], cot_theirs.at[target], sems.at[1 + r]))
    for copy in copies:
        copy.wait()


def gradient(position, scaled0, scaled1, exch0, exch1, grad0, grad, staged, sems):
    core, column, y, rows = position[0], position[1], position[2], position[3]
    step = 2 * core - 1
    places = [lax.rem(y + d + rows, rows) for d in (0, step, 2, -step)]
    copies = []
    for g, place in enumerate(places):
        target = grad.at[pl.ds((column * rows + place) * 2, 2)]
        copies += started(pltpu.make_async_copy(grad0.at[pl.ds(2 * g, 2)], target, sems.at[g]))

    def store(group, h, block):
        staged[2 * group + h] = block
        if h == 1:
            target = grad.at[pl.ds(((1 - column) * rows + places[group]) * 2, 2)]
            copies.extend(started(pltpu.make_async_copy(staged.at[pl.ds(2 * group, 2)], target, sems.at[4 + group])))

    reduce_walkers(terms_of(scaled0, exch0) + terms_of(scaled1, exch1), store)
    for copy in copies:
        copy.wait()


def finish(early0, late0, vectors0, early1, late1, vectors1, returned, *refs):
    outs, (exch, vectors, staged, sems, out_sems) = refs[:-5], refs[-5:]
    o = outs[0].shape[0]
    split = early0.shape[0]
    cuts = [0, 4 * o, 8 * o]
    pieces = []
    count = 2
    for lo, hi in zip(cuts, cuts[1:]):
        both = []
        for h, (early_rows, late_rows) in enumerate(((early0, late0), (early1, late1))):
            piece = []
            for source, at, a, b in ((early_rows, 0, lo, min(hi, split)), (late_rows, split, max(lo, split), hi)):
                if a < b:
                    rows = pl.ds(a, b - a)
                    piece.append(
                        pltpu.make_async_copy(source.at[pl.ds(a - at, b - a)], exch.at[h, rows], sems.at[count])
                    )
                    count += 1
            both.append(piece)
        pieces.append(both)
    load0 = started(pltpu.make_async_copy(vectors0, vectors.at[0], sems.at[0]))[0]
    started(*pieces[0][0])
    load1 = started(pltpu.make_async_copy(vectors1, vectors.at[1], sems.at[1]))[0]
    started(*pieces[0][1])
    for piece, other in pieces[1:]:
        started(*piece, *other)
    load0.wait()
    stores = []
    for r, (piece, other) in enumerate(pieces):
        lo, hi = cuts[r], cuts[r + 1]
        for copy in piece:
            copy.wait()
        part = jnp.dot(exch[0, lo:hi, :], vectors[0], preferred_element_type=F32)
        if r == 0:
            load1.wait()
        for copy in other:
            copy.wait()
        part += jnp.dot(exch[1, lo:hi, :], vectors[1], preferred_element_type=F32)
        part += returned[lo:hi, :].astype(F32)
        for w in range((hi - lo) // o):
            k = lo // o + w
            staged[k] = part[w * o : (w + 1) * o, :].astype(BF16)
            stores += started(pltpu.make_async_copy(staged.at[k], outs[k], out_sems.at[k]))
    for copy in stores:
        copy.wait()


def total(position, parts, keep, send):
    core = position[0]
    rows = keep.shape[0]
    for out, c in ((send, 1 - core), (keep, core)):
        start = pl.multiple_of(c * rows, rows)
        acc = parts[0, pl.ds(start, rows), :].astype(F32)
        for s in range(1, parts.shape[0]):
            acc += parts[s, pl.ds(start, rows), :].astype(F32)
        out[...] = -acc


def place(position, keep, received, out):
    core = position[0]
    n = out.shape[1]
    for h in range(2):
        out[2 * h + core] = keep[:, h * n : (h + 1) * n].T
        out[2 * h + 1 - core] = received[:, h * n : (h + 1) * n].T


def step(green, vectors, weight):
    zs, ys = lax.axis_size("z"), lax.axis_size("y")
    plane = lax.axis_size("xl") * ys * lax.axis_size("xh")
    _, o, m = green.shape
    index = [lax.axis_index(a) for a in ("core", "xl", "y")]
    position = jnp.stack([*index, jnp.int32(ys)]).astype(jnp.int32)
    shape = jax.ShapeDtypeStruct
    dma = pltpu.SemaphoreType.DMA

    payload, ordered = call(
        prepare,
        (pltpu.VMEM((1, o + EXTRA, m), BF16), pltpu.VMEM((4, o, m), BF16)),
        [SMEM, SMEM, HBM, HBM],
        8,
        scratch=[dma((5,))],
    )(position, weight, hold(green), hold(vectors))

    y1 = opposed(ordered, "y", 1)
    chip = jnp.concatenate([payload, swap(payload)])
    z2 = opposed(chip, "z", 2)
    z1 = opposed(chip, "z", 1)
    x0 = opposed(ordered[:2], "x", 1)
    y2 = opposed(y1[:2], "y", 1)
    x1 = opposed(y1, "x", 1)
    y3 = swap(y1[2:])
    z3 = opposed(z2, "z", 1)
    z4 = opposed(z2[:1], "z", 2)
    near = jnp.concatenate([z1, z2])
    w1 = swap(near)
    x2 = opposed(y2, "x", 1)
    x3 = swap(x1[2:])
    rest = jnp.concatenate([z3, z4])
    w2 = swap(rest)

    half = plane // 2
    pair_flops = 2 * o * o * m
    ne, nl = len(EARLY_MINE), len(LATE_MINE)
    exch0, scaled0, vectors0, kept_early, kept_vectors0 = call(
        early,
        (
            pltpu.VMEM((2 * ne * o, half * o), BF16),
            pltpu.VMEM((ne, m, 2 * o), BF16),
            pltpu.VMEM((half * o, m), BF16),
            pltpu.HBM((ne * o, half * o), BF16),
            pltpu.HBM((half * o, m), BF16),
        ),
        [VMEM] * 7,
        20,
        flops=2 * ne * half * pair_flops,
        scratch=[dma((2,))],
        out_specs=(VMEM,) * 3 + (HBM,) * 2,
    )(chip, near, w1, ordered, y1, y2, y3)

    exch1, scaled1, grad0, kept_late = call(
        first,
        (
            pltpu.VMEM((2 * nl * o, half * o), BF16),
            pltpu.VMEM((nl, m, 2 * o), BF16),
            pltpu.VMEM((half, m // 2, 2 * o), BF16),
            pltpu.HBM((nl * o, half * o), BF16),
        ),
        [VMEM] * 5,
        24,
        flops=2 * zs * plane * pair_flops,
        scratch=[dma((1,))],
        out_specs=(VMEM,) * 3 + (HBM,),
    )(rest, w2, exch0, scaled0, vectors0)

    exch2, vectors1, kept_early1, kept_vectors1 = call(
        beyond,
        (
            pltpu.VMEM((2 * ne * o, half * o), BF16),
            pltpu.VMEM((half * o, m), BF16),
            pltpu.HBM((ne * o, half * o), BF16),
            pltpu.HBM((half * o, m), BF16),
        ),
        [VMEM] * 7,
        20,
        flops=2 * ne * half * pair_flops,
        scratch=[dma((2,))],
        out_specs=(VMEM,) * 2 + (HBM,) * 2,
    )(chip, near, w1, x0, x1, x2, x3)

    exch3, cot_theirs, kept_late1 = call(
        second,
        (
            pltpu.VMEM((2 * nl * o, half * o), BF16),
            pltpu.HBM((zs * o, m), BF16),
            pltpu.HBM((nl * o, half * o), BF16),
        ),
        [VMEM] * 7,
        24,
        flops=2 * zs * plane * pair_flops,
        scratch=[pltpu.VMEM((zs * o, m), BF16), dma((3,))],
        out_specs=(VMEM,) + (HBM,) * 2,
    )(rest, w2, exch0, exch1, exch2, vectors0, vectors1)
    returned = swap(cot_theirs)

    grad = call(
        gradient,
        pltpu.HBM((plane, m // 2, 2 * o), BF16),
        [SMEM] + [VMEM] * 5,
        24,
        flops=zs * plane * pair_flops,
        scratch=[pltpu.VMEM((half, m // 2, 2 * o), BF16), dma((8,))],
        out_specs=HBM,
    )(position, scaled0, scaled1, exch2, exch3, grad0)

    grad = lax.all_to_all(grad, PLANE, 0, 0, tiled=True)
    sums = call(
        finish,
        tuple(pltpu.HBM((o, m), BF16) for _ in range(zs)),
        [HBM] * 6 + [VMEM],
        24,
        flops=zs * plane * pair_flops,
        scratch=[
            pltpu.VMEM((2, zs * o, half * o), BF16),
            pltpu.VMEM((2, half * o, m), BF16),
            pltpu.VMEM((zs, o, m), BF16),
            dma((14,)),
            dma((zs,)),
        ],
        out_specs=(HBM,) * zs,
    )(*(hold(x) for x in (kept_early, kept_late, kept_vectors0, kept_early1, kept_late1, kept_vectors1)), returned)
    cot = None
    for k, block in sorted(zip(OFFSETS, sums), key=lambda kb: -abs(kb[0])):
        part = (block if k == 0 else opposed(block, "z", -k)).astype(F32)
        cot = part if cot is None else cot + part
    minus = -weight[0]
    green_cot = (minus * cot)[None]

    keep, send = call(total, (shape((m // 4, 2 * o), F32),) * 2, [SMEM, VMEM], 16)(position, grad)
    chol_grad = call(place, shape((4, o, m // 4), F32), [SMEM, VMEM, VMEM], 16)(position, keep, swap(send))
    return green_cot, chol_grad


def solution(mesh):
    grid = Mesh(mesh.devices.reshape(2, 8, 4, 2, 2), AXES)
    chol, walk = ("xl", "z", "y"), ("xh", "core")
    every = chol + walk
    return jax.shard_map(
        step,
        mesh=grid,
        in_specs=(P(every, None, None), P(chol, None, None), P(every)),
        out_specs=(P(every, None, None), P(chol, None, walk)),
        check_vma=False,
    )
```

```python
import jax
import jax.numpy as jnp
from jax import lax
from jax.experimental import pallas as pl
from jax.experimental.pallas import tpu as pltpu
from jax.sharding import Mesh, PartitionSpec as P


F32 = jnp.float32
BF16 = jnp.bfloat16
AXES = ("xl", "z", "y", "xh", "core")
PLANE = ("xl", "y", "xh")
VMEM = pl.BlockSpec(memory_space=pltpu.VMEM)
HBM = pl.BlockSpec(memory_space=pltpu.HBM)
SMEM = pl.BlockSpec(memory_space=pltpu.SMEM)
EXTRA = 16
EARLY_MINE = ((0, 0), (1, 0), (1, 2), (3, 1), (3, 3))
EARLY_THEIRS = ((0, 1), (3, 0), (3, 2), (1, 1), (1, 3))
LATE_MINE = ((2, 0), (2, 2), (4, 1))
LATE_THEIRS = ((4, 0), (4, 2), (2, 1))
OFFSETS = (0, 1, 2, -1, -2, 3, 4, -3)


def opposed(block, axis, distance):
    if axis == "x":
        n = lax.axis_size("xl") * lax.axis_size("xh")
        flat = [(x % 2) * (n // 2) + x // 2 for x in range(n)]
        names = ("xl", "xh", "core")
    else:
        n = lax.axis_size(axis)
        flat = list(range(n))
        names = (axis, "core")
    route = []
    for i in range(n):
        route.append((2 * flat[i], 2 * flat[(i + distance) % n]))
        route.append((2 * flat[i] + 1, 2 * flat[(i - distance) % n] + 1))
    return lax.ppermute(block, names, route)


def swap(block):
    return lax.ppermute(block, "core", [(0, 1), (1, 0)])


def hold(x):
    return pltpu.with_memory_space_constraint(x, pltpu.HBM)


def call(body, outs, ins, mib, flops=0, moved=2 << 20, scratch=(), out_specs=None):
    return pl.pallas_call(
        body,
        out_shape=outs,
        in_specs=ins,
        out_specs=jax.tree.map(lambda _: VMEM, outs) if out_specs is None else out_specs,
        scratch_shapes=scratch,
        compiler_params=pltpu.CompilerParams(vmem_limit_bytes=mib << 20),
        cost_estimate=pl.CostEstimate(flops=flops, bytes_accessed=moved, transcendentals=0),
    )


def prepare(position, weight, green, vectors, payload, ordered, sems):
    core = position[0]
    o, m = green.shape[1:]
    copies = [pltpu.make_async_copy(green, payload.at[:, pl.ds(0, o)], sems.at[4])]
    for k, v in enumerate((core, core + 2, 1 - core, 3 - core)):
        copies.append(pltpu.make_async_copy(vectors.at[v], ordered.at[k], sems.at[k]))
    for copy in copies:
        copy.start()
    w = jnp.full((EXTRA, m), weight[0], F32)
    high = w.astype(BF16).astype(F32)
    middle = (w - high).astype(BF16).astype(F32)
    low = w - high - middle
    row = lax.broadcasted_iota(jnp.int32, w.shape, 0)
    tile = jnp.where(row == 0, high, jnp.where(row == 1, middle, jnp.where(row == 2, low, 0.0)))
    payload[0, o:, :] = tile.astype(BF16)
    for copy in copies:
        copy.wait()


def collect(groups, vectors):
    o, _ = groups[0].shape[1:]
    for g, group in enumerate(groups):
        for j in range(2):
            vectors[(2 * g + j) * o : (2 * g + j + 1) * o, :] = group[j]


def multiply(vectors, walkers, places, exch, base=0, scaled=None):
    o = vectors.shape[0] // 8
    quad = 4
    for i in range(len(places) // 2):
        pair = places[2 * i : 2 * i + 2]
        blocks = [walkers[a][k, :o, :] for a, k in pair]
        both = jnp.concatenate(blocks)
        for q in range(2):
            part = lax.dot_general(
                vectors[q * quad * o : (q + 1) * quad * o, :],
                both,
                (((1,), (1,)), ((), ())),
                preferred_element_type=F32,
            ).astype(BF16)
            for g in range(quad):
                for w in range(2):
                    row = base + (2 * i + w) * o
                    exch[row : row + o, (q * quad + g) * o : (q * quad + g + 1) * o] = part[
                        g * o : (g + 1) * o, w * o : (w + 1) * o
                    ]
        if scaled is not None:
            for w, (a, k) in enumerate(pair):
                weight = jnp.sum(walkers[a][k, o:, :].astype(F32), axis=0, keepdims=True)
                scaled[i, :, w * o : (w + 1) * o] = (blocks[w].astype(F32) * weight).astype(BF16).T


def reduce_walkers(terms, store):
    scaled, _, exch, _ = terms[0]
    _, m, two = scaled.shape
    width = two
    for c in range(exch.shape[1] // width):
        acc = jnp.zeros((m, width), F32)
        for scaled, i, exch, row in terms:
            acc += jnp.dot(
                scaled[i], exch[row : row + two, c * width : (c + 1) * width], preferred_element_type=F32
            )
        acc = acc.astype(BF16)
        for s in range(width // two):
            for h in range(2):
                store(c * (width // two) + s, h, acc[h * m // 2 : (h + 1) * m // 2, s * two : (s + 1) * two])


def terms_of(scaled, exch):
    two = scaled.shape[2]
    return [(scaled, i, exch, i * two) for i in range(scaled.shape[0])]


def started(*copies):
    for copy in copies:
        copy.start()
    return list(copies)


def early(chip, near, w1, v0, v1, v2, v3, exch, scaled, vectors, kept_exch, kept_vectors, sems):
    collect((v0, v1, v2, v3), vectors)
    copies = started(pltpu.make_async_copy(vectors, kept_vectors, sems.at[0]))
    multiply(vectors, {0: chip, 1: near, 3: w1}, EARLY_MINE + EARLY_THEIRS, exch, scaled=scaled)
    rows = kept_exch.shape[0]
    copies += started(pltpu.make_async_copy(exch.at[pl.ds(0, rows)], kept_exch, sems.at[1]))
    for copy in copies:
        copy.wait()


def first(rest, w2, exch0, scaled0, vectors, exch, scaled, grad, kept_exch, sems):
    multiply(vectors, {2: rest, 4: w2}, LATE_MINE + LATE_THEIRS, exch, scaled=scaled)
    rows = kept_exch.shape[0]
    copies = started(pltpu.make_async_copy(exch.at[pl.ds(0, rows)], kept_exch, sems.at[0]))

    def store(group, h, block):
        grad[2 * group + h] = block

    reduce_walkers(terms_of(scaled0, exch0) + terms_of(scaled, exch), store)
    for copy in copies:
        copy.wait()


def beyond(chip, near, w1, v0, v1, v2, v3, exch, vectors, kept_exch, kept_vectors, sems):
    collect((v0, v1, v2, v3), vectors)
    copies = started(pltpu.make_async_copy(vectors, kept_vectors, sems.at[0]))
    multiply(vectors, {0: chip, 1: near, 3: w1}, EARLY_MINE + EARLY_THEIRS, exch)
    rows = kept_exch.shape[0]
    copies += started(pltpu.make_async_copy(exch.at[pl.ds(0, rows)], kept_exch, sems.at[1]))
    for copy in copies:
        copy.wait()


def second(rest, w2, exch0, exch1, exch2, vectors0, vectors1, exch, cot_theirs, kept_exch, cot, sems):
    multiply(vectors1, {2: rest, 4: w2}, LATE_MINE + LATE_THEIRS, exch)
    split, count = exch0.shape[0] // 2, exch1.shape[0] // 2
    copies = started(pltpu.make_async_copy(exch.at[pl.ds(0, count)], kept_exch, sems.at[0]))
    for r, (own, other, size) in enumerate(((exch0, exch2, split), (exch1, exch, count))):
        target = slice(r * split, r * split + size)
        part = jnp.dot(own[size : 2 * size, :], vectors0[...], preferred_element_type=F32)
        part += jnp.dot(other[size : 2 * size, :], vectors1[...], preferred_element_type=F32)
        cot[target, :] = part.astype(BF16)
        copies += started(pltpu.make_async_copy(cot.at[target], cot_theirs.at[target], sems.at[1 + r]))
    for copy in copies:
        copy.wait()


def gradient(position, scaled0, scaled1, exch0, exch1, grad0, grad, staged, sems):
    core, column, y, rows = position[0], position[1], position[2], position[3]
    step = 2 * core - 1
    places = [lax.rem(y + d + rows, rows) for d in (0, step, 2, -step)]
    copies = []
    for g, place in enumerate(places):
        target = grad.at[pl.ds((column * rows + place) * 2, 2)]
        copies += started(pltpu.make_async_copy(grad0.at[pl.ds(2 * g, 2)], target, sems.at[g]))

    def store(group, h, block):
        staged[2 * group + h] = block
        if h == 1:
            target = grad.at[pl.ds(((1 - column) * rows + places[group]) * 2, 2)]
            copies.extend(started(pltpu.make_async_copy(staged.at[pl.ds(2 * group, 2)], target, sems.at[4 + group])))

    reduce_walkers(terms_of(scaled0, exch0) + terms_of(scaled1, exch1), store)
    for copy in copies:
        copy.wait()


def finish(early0, late0, vectors0, early1, late1, vectors1, returned, *refs):
    outs, (exch, vectors, staged, sems, out_sems) = refs[:-5], refs[-5:]
    o = outs[0].shape[0]
    split = early0.shape[0]
    cuts = [0, 4 * o, 8 * o]
    pieces = []
    count = 2
    for lo, hi in zip(cuts, cuts[1:]):
        both = []
        for h, (early_rows, late_rows) in enumerate(((early0, late0), (early1, late1))):
            piece = []
            for source, at, a, b in ((early_rows, 0, lo, min(hi, split)), (late_rows, split, max(lo, split), hi)):
                if a < b:
                    rows = pl.ds(a, b - a)
                    piece.append(
                        pltpu.make_async_copy(source.at[pl.ds(a - at, b - a)], exch.at[h, rows], sems.at[count])
                    )
                    count += 1
            both.append(piece)
        pieces.append(both)
    load0 = started(pltpu.make_async_copy(vectors0, vectors.at[0], sems.at[0]))[0]
    started(*pieces[0][0])
    load1 = started(pltpu.make_async_copy(vectors1, vectors.at[1], sems.at[1]))[0]
    started(*pieces[0][1])
    for piece, other in pieces[1:]:
        started(*piece, *other)
    load0.wait()
    stores = []
    for r, (piece, other) in enumerate(pieces):
        lo, hi = cuts[r], cuts[r + 1]
        for copy in piece:
            copy.wait()
        part = jnp.dot(exch[0, lo:hi, :], vectors[0], preferred_element_type=F32)
        if r == 0:
            load1.wait()
        for copy in other:
            copy.wait()
        part += jnp.dot(exch[1, lo:hi, :], vectors[1], preferred_element_type=F32)
        part += returned[lo:hi, :].astype(F32)
        for w in range((hi - lo) // o):
            k = lo // o + w
            staged[k] = part[w * o : (w + 1) * o, :].astype(BF16)
            stores += started(pltpu.make_async_copy(staged.at[k], outs[k], out_sems.at[k]))
    for copy in stores:
        copy.wait()


def total(position, parts, keep, send):
    core = position[0]
    rows = keep.shape[2]
    n = keep.shape[1]
    for out, c in ((send, 1 - core), (keep, core)):
        start = pl.multiple_of(c * rows, rows)
        acc = parts[0, pl.ds(start, rows), :].astype(F32)
        for s in range(1, parts.shape[0]):
            acc += parts[s, pl.ds(start, rows), :].astype(F32)
        for h in range(2):
            out[h] = -acc[:, h * n : (h + 1) * n].T


def place(position, keep, received, out, sems):
    core = position[0]
    copies = []
    for h in range(2):
        copies += started(
            pltpu.make_async_copy(keep.at[h], out.at[2 * h + core], sems.at[2 * h]),
            pltpu.make_async_copy(received.at[h], out.at[2 * h + 1 - core], sems.at[2 * h + 1]),
        )
    for copy in copies:
        copy.wait()


def step(green, vectors, weight):
    zs, ys = lax.axis_size("z"), lax.axis_size("y")
    plane = lax.axis_size("xl") * ys * lax.axis_size("xh")
    _, o, m = green.shape
    index = [lax.axis_index(a) for a in ("core", "xl", "y")]
    position = jnp.stack([*index, jnp.int32(ys)]).astype(jnp.int32)
    shape = jax.ShapeDtypeStruct
    dma = pltpu.SemaphoreType.DMA

    payload, ordered = call(
        prepare,
        (pltpu.VMEM((1, o + EXTRA, m), BF16), pltpu.VMEM((4, o, m), BF16)),
        [SMEM, SMEM, HBM, HBM],
        8,
        scratch=[dma((5,))],
    )(position, weight, hold(green), hold(vectors))

    y1 = opposed(ordered, "y", 1)
    chip = jnp.concatenate([payload, swap(payload)])
    z2 = opposed(chip, "z", 2)
    z1 = opposed(chip, "z", 1)
    x0 = opposed(ordered[:2], "x", 1)
    y2 = opposed(y1[:2], "y", 1)
    x1 = opposed(y1, "x", 1)
    y3 = swap(y1[2:])
    z3 = opposed(z2, "z", 1)
    z4 = opposed(z2[:1], "z", 2)
    near = jnp.concatenate([z1, z2])
    w1 = swap(near)
    x2 = opposed(y2, "x", 1)
    x3 = swap(x1[2:])
    rest = jnp.concatenate([z3, z4])
    w2 = swap(rest)

    half = plane // 2
    pair_flops = 2 * o * o * m
    ne, nl = len(EARLY_MINE), len(LATE_MINE)
    exch0, scaled0, vectors0, kept_early, kept_vectors0 = call(
        early,
        (
            pltpu.VMEM((2 * ne * o, half * o), BF16),
            pltpu.VMEM((ne, m, 2 * o), BF16),
            pltpu.VMEM((half * o, m), BF16),
            pltpu.HBM((ne * o, half * o), BF16),
            pltpu.HBM((half * o, m), BF16),
        ),
        [VMEM] * 7,
        20,
        flops=2 * ne * half * pair_flops,
        scratch=[dma((2,))],
        out_specs=(VMEM,) * 3 + (HBM,) * 2,
    )(chip, near, w1, ordered, y1, y2, y3)

    exch1, scaled1, grad0, kept_late = call(
        first,
        (
            pltpu.VMEM((2 * nl * o, half * o), BF16),
            pltpu.VMEM((nl, m, 2 * o), BF16),
            pltpu.VMEM((half, m // 2, 2 * o), BF16),
            pltpu.HBM((nl * o, half * o), BF16),
        ),
        [VMEM] * 5,
        24,
        flops=2 * zs * plane * pair_flops,
        scratch=[dma((1,))],
        out_specs=(VMEM,) * 3 + (HBM,),
    )(rest, w2, exch0, scaled0, vectors0)

    exch2, vectors1, kept_early1, kept_vectors1 = call(
        beyond,
        (
            pltpu.VMEM((2 * ne * o, half * o), BF16),
            pltpu.VMEM((half * o, m), BF16),
            pltpu.HBM((ne * o, half * o), BF16),
            pltpu.HBM((half * o, m), BF16),
        ),
        [VMEM] * 7,
        20,
        flops=2 * ne * half * pair_flops,
        scratch=[dma((2,))],
        out_specs=(VMEM,) * 2 + (HBM,) * 2,
    )(chip, near, w1, x0, x1, x2, x3)

    exch3, cot_theirs, kept_late1 = call(
        second,
        (
            pltpu.VMEM((2 * nl * o, half * o), BF16),
            pltpu.HBM((zs * o, m), BF16),
            pltpu.HBM((nl * o, half * o), BF16),
        ),
        [VMEM] * 7,
        24,
        flops=2 * zs * plane * pair_flops,
        scratch=[pltpu.VMEM((zs * o, m), BF16), dma((3,))],
        out_specs=(VMEM,) + (HBM,) * 2,
    )(rest, w2, exch0, exch1, exch2, vectors0, vectors1)
    returned = swap(cot_theirs)

    grad = call(
        gradient,
        pltpu.HBM((plane, m // 2, 2 * o), BF16),
        [SMEM] + [VMEM] * 5,
        24,
        flops=zs * plane * pair_flops,
        scratch=[pltpu.VMEM((half, m // 2, 2 * o), BF16), dma((8,))],
        out_specs=HBM,
    )(position, scaled0, scaled1, exch2, exch3, grad0)

    grad = lax.all_to_all(grad, PLANE, 0, 0, tiled=True)
    sums = call(
        finish,
        tuple(pltpu.HBM((o, m), BF16) for _ in range(zs)),
        [HBM] * 6 + [VMEM],
        24,
        flops=zs * plane * pair_flops,
        scratch=[
            pltpu.VMEM((2, zs * o, half * o), BF16),
            pltpu.VMEM((2, half * o, m), BF16),
            pltpu.VMEM((zs, o, m), BF16),
            dma((14,)),
            dma((zs,)),
        ],
        out_specs=(HBM,) * zs,
    )(*(hold(x) for x in (kept_early, kept_late, kept_vectors0, kept_early1, kept_late1, kept_vectors1)), returned)
    cot = None
    for k, block in sorted(zip(OFFSETS, sums), key=lambda kb: -abs(kb[0])):
        part = (block if k == 0 else opposed(block, "z", -k)).astype(F32)
        cot = part if cot is None else cot + part
    minus = -weight[0]
    green_cot = (minus * cot)[None]

    keep, send = call(total, (shape((2, o, m // 4), F32),) * 2, [SMEM, VMEM], 16)(position, grad)
    chol_grad = call(
        place, pltpu.HBM((4, o, m // 4), F32), [SMEM, VMEM, VMEM], 16, scratch=[dma((4,))], out_specs=HBM
    )(position, keep, swap(send))
    return green_cot, chol_grad


def solution(mesh):
    grid = Mesh(mesh.devices.reshape(2, 8, 4, 2, 2), AXES)
    chol, walk = ("xl", "z", "y"), ("xh", "core")
    every = chol + walk
    return jax.shard_map(
        step,
        mesh=grid,
        in_specs=(P(every, None, None), P(chol, None, None), P(every)),
        out_specs=(P(every, None, None), P(chol, None, walk)),
        check_vma=False,
    )
```
